32 devices in a mesh: groups: 2 (over x), space: 16 (over z, y, core).
Axes of the slice: x: 2, y: 2, z: 4, core: 2. Of those that a mesh axis runs over, the one named last changes fastest.
Arguments:
- lifted_field: float32 [64, 16, 128, 256], P('groups', 'space'), parts along dimension 0, may hold values from -6 to 6
- cotangent: bfloat16 [64, 16, 128, 256], P('groups', 'space'), parts along dimension 0, may hold values from -6 to 6
- spectral_weights: float32 [2, 32, 1024, 32, 32], P(None, None, 'space'), may hold values from -4 to 4
- point_weights: float32 [32, 32], replicated, may hold values from -1 to 1
- point_bias: float32 [32], replicated, may hold values from -3 to 3
Outputs:
- activated: bfloat16 [64, 16, 128, 256], P('groups', 'space'), parts along dimension 0
- grad_spectral: float32 [4, 32, 1024, 32, 32], P('groups', None, 'space'), parts along dimension 0
- grad_point: float32 [64, 32], P('groups'), parts along dimension 0
- grad_bias: float32 [64], P('groups'), parts along dimension 0
The draws below stay inside these ranges and needn't reach their ends.
There are 2 independent parts, one for each index of `groups`. The reference program is written for one: setup_inputs(seed, part) draws one part's arguments, and reference() takes and returns one part's arrays. A program takes and returns all parts, laid end to end along the dimension named above; an argument that names none is the same for every part. Nothing has to cross between parts.
All inputs are finite; a program needn't handle non-finite values.
Results may differ from the reference program's by a relative error of at most 0.001.
Values sent between devices are 32-bit elements; how exact they have to be, the bound alone decides.
A program may use at most 192 MiB of HBM per device.

```python
import jax
import jax.numpy as jnp
from jax import lax

C = 32
MX = 32
MY = 32
MZ = 32
NY = 128
NZ = 256
NX = 16
MODES = 1024


def block_levels(own_key, shape, split, smallest, top_value):
    level = 1.0
    for axis_at, shards_of in split:
        steps = jax.random.uniform(jax.random.fold_in(jax.random.fold_in(own_key, 6), axis_at), (shards_of,), jnp.float32, smallest / len(split), top_value / len(split))
        level = level * jnp.repeat(jnp.exp(steps), shape[axis_at] // shards_of).reshape((-1,) + (1,) * (len(shape) - 1 - axis_at))
    return level


def centred(stream_key, extent, scale, most, split=(), kind=jnp.bfloat16):
    loudness = block_levels(stream_key, extent, split, -0.22, 0.18) if split else 1.0
    values = jax.random.normal(stream_key, extent, jnp.float32) * scale * loudness
    return jnp.minimum(jnp.maximum(values, -most), most).astype(kind)


def setup_inputs(seed: int = 0, part: int = 0) -> dict:
    streams_of = jax.random.split(jax.random.key(seed), 6)
    part_keys = jax.random.split(jax.random.fold_in(streams_of[5], part), 6)
    lifted_field = centred(part_keys[0], (C, NX, NY, NZ), 1.0, 6.0, ((1, 16),), jnp.float32)
    cotangent = centred(part_keys[1], (C, NX, NY, NZ), 1.0, 6.0, ((1, 16),))
    spectral_weights = centred(streams_of[2], (2, MX, MODES, C, C), (C // 16) ** -0.5, 4.0, ((2, 16),), jnp.float32)
    point_weights = centred(streams_of[3], (C, C), C ** -0.5, 1.0, (), jnp.float32)
    point_bias = centred(streams_of[4], (C,), 0.5, 3.0, (), jnp.float32)
    return {"lifted_field": lifted_field, "cotangent": cotangent, "spectral_weights": spectral_weights, "point_weights": point_weights, "point_bias": point_bias}


HIGHEST = lax.Precision.HIGHEST
INV_SQRT_TWO = 0.7071067811865476
INV_SQRT_TWO_PI = 0.3989422804014327


def trig_tables(positions, frequency, length):
    product = (positions[:, None] * frequency[None, :]) % length
    phase_angle = (2.0 * jnp.pi / length) * product.astype(jnp.float32)
    return jnp.cos(phase_angle), jnp.sin(phase_angle)


def kept_frequencies(kept_count, length):
    mode_index = jnp.arange(kept_count, dtype=jnp.int32)
    return jnp.where(mode_index < kept_count // 2, mode_index, length - kept_count + mode_index).astype(jnp.int32)


def forward_local(field_in):
    channels = field_in.shape[0]
    width_x = field_in.shape[1]
    cos_z, sin_z = trig_tables(jnp.arange(NZ, dtype=jnp.int32), jnp.arange(MZ, dtype=jnp.int32), NZ)
    table_z = jnp.concatenate([cos_z, -sin_z], axis=1)
    along_z = jnp.einsum("cxyz,zk->cxyk", field_in, table_z, precision=HIGHEST)
    z_real = along_z[..., :MZ]
    z_imag = along_z[..., MZ:]
    cos_y, sin_y = trig_tables(jnp.arange(NY, dtype=jnp.int32), kept_frequencies(MY, NY), NY)
    y_real = jnp.einsum("cxyk,yj->xcjk", z_real, cos_y, precision=HIGHEST) + jnp.einsum("cxyk,yj->xcjk", z_imag, sin_y, precision=HIGHEST)
    y_imag = jnp.einsum("cxyk,yj->xcjk", z_imag, cos_y, precision=HIGHEST) - jnp.einsum("cxyk,yj->xcjk", z_real, sin_y, precision=HIGHEST)
    stacked = jnp.stack([y_real, y_imag], axis=1)
    return stacked.reshape(width_x, 2, channels, MY * MZ)


def transform_x(x_lines):
    length_x = x_lines.shape[0]
    cos_x, sin_x = trig_tables(jnp.arange(length_x, dtype=jnp.int32), kept_frequencies(MX, length_x), length_x)
    norm_scale = 1.0 / (float(length_x * NY * NZ) ** 0.5)
    part_real = x_lines[:, 0]
    part_imag = x_lines[:, 1]
    x_real = jnp.einsum("xcm,xk->kcm", part_real, cos_x, precision=HIGHEST) + jnp.einsum("xcm,xk->kcm", part_imag, sin_x, precision=HIGHEST)
    x_imag = jnp.einsum("xcm,xk->kcm", part_imag, cos_x, precision=HIGHEST) - jnp.einsum("xcm,xk->kcm", part_real, sin_x, precision=HIGHEST)
    return norm_scale * jnp.stack([x_real, x_imag], axis=1)


def mix_modes(spectrum, weights):
    spec_real = spectrum[:, 0]
    spec_imag = spectrum[:, 1]
    out_real = jnp.einsum("kim,kmio->kom", spec_real, weights[0], precision=HIGHEST) - jnp.einsum("kim,kmio->kom", spec_imag, weights[1], precision=HIGHEST)
    out_imag = jnp.einsum("kim,kmio->kom", spec_real, weights[1], precision=HIGHEST) + jnp.einsum("kim,kmio->kom", spec_imag, weights[0], precision=HIGHEST)
    return jnp.stack([out_real, out_imag], axis=1)


def inverse_x(spectrum, positions, length_x):
    cos_x, sin_x = trig_tables(positions, kept_frequencies(MX, length_x), length_x)
    spec_real = spectrum[:, 0]
    spec_imag = spectrum[:, 1]
    a_real = jnp.einsum("kcm,xk->xcm", spec_real, cos_x, precision=HIGHEST) - jnp.einsum("kcm,xk->xcm", spec_imag, sin_x, precision=HIGHEST)
    a_imag = jnp.einsum("kcm,xk->xcm", spec_imag, cos_x, precision=HIGHEST) + jnp.einsum("kcm,xk->xcm", spec_real, sin_x, precision=HIGHEST)
    return jnp.stack([a_real, a_imag], axis=1)


def inverse_yz(x_lines, length_x):
    width_x = x_lines.shape[0]
    channels = x_lines.shape[2]
    mode_grid = x_lines.reshape(width_x, 2, channels, MY, MZ)
    cos_y, sin_y = trig_tables(jnp.arange(NY, dtype=jnp.int32), kept_frequencies(MY, NY), NY)
    b_real = jnp.einsum("xcjk,yj->cxyk", mode_grid[:, 0], cos_y, precision=HIGHEST) - jnp.einsum("xcjk,yj->cxyk", mode_grid[:, 1], sin_y, precision=HIGHEST)
    b_imag = jnp.einsum("xcjk,yj->cxyk", mode_grid[:, 1], cos_y, precision=HIGHEST) + jnp.einsum("xcjk,yj->cxyk", mode_grid[:, 0], sin_y, precision=HIGHEST)
    cos_z, sin_z = trig_tables(jnp.arange(NZ, dtype=jnp.int32), jnp.arange(MZ, dtype=jnp.int32), NZ)
    weight_z = jnp.where(jnp.arange(MZ, dtype=jnp.int32) == 0, 1.0, 2.0).astype(jnp.float32)
    table_z = jnp.concatenate([cos_z * weight_z[None, :], -sin_z * weight_z[None, :]], axis=1)
    stacked = jnp.concatenate([b_real, b_imag], axis=-1)
    result = jnp.einsum("cxyk,zk->cxyz", stacked, table_z, precision=HIGHEST)
    return result * (1.0 / (float(length_x * NY * NZ) ** 0.5))


def gelu_slope(values):
    return 0.5 * (1.0 + lax.erf(values * INV_SQRT_TWO)) + values * jnp.exp(-0.5 * values * values) * INV_SQRT_TWO_PI


def weight_gradient(spectrum, slope_modes, first_mode):
    mode_ids = first_mode + jnp.arange(spectrum.shape[3], dtype=jnp.int32)
    weight_modes = jnp.where(mode_ids % MZ == 0, 1.0, 2.0).astype(jnp.float32)
    grad_real = jnp.einsum("kim,kom->kmio", spectrum[:, 0], slope_modes[:, 0], precision=HIGHEST) + jnp.einsum("kim,kom->kmio", spectrum[:, 1], slope_modes[:, 1], precision=HIGHEST)
    grad_imag = jnp.einsum("kim,kom->kmio", spectrum[:, 0], slope_modes[:, 1], precision=HIGHEST) - jnp.einsum("kim,kom->kmio", spectrum[:, 1], slope_modes[:, 0], precision=HIGHEST)
    stacked = jnp.stack([grad_real, grad_imag], axis=0)
    return stacked * weight_modes[None, None, :, None, None]


def reference(lifted_field, cotangent, spectral_weights, point_weights, point_bias):
    length_x = lifted_field.shape[1]
    spectrum = transform_x(forward_local(lifted_field))
    mixed_modes = mix_modes(spectrum, spectral_weights)
    x_lines = inverse_x(mixed_modes, jnp.arange(length_x, dtype=jnp.int32), length_x)
    spectral = inverse_yz(x_lines, length_x)
    pointwise = jnp.einsum("ixyz,io->oxyz", lifted_field, point_weights, precision=HIGHEST) + point_bias[:, None, None, None]
    before = spectral + pointwise
    activated = jax.nn.gelu(before, approximate=False).astype(jnp.bfloat16)
    slope_field = cotangent.astype(jnp.float32) * gelu_slope(before)
    root_cells = float(length_x * NY * NZ) ** 0.5
    grad_point = jnp.einsum("ixyz,oxyz->io", lifted_field, slope_field, precision=HIGHEST) / root_cells
    grad_bias = jnp.sum(slope_field, axis=(1, 2, 3)) / root_cells
    slope_spectrum = transform_x(forward_local(slope_field))
    grad_spectral = weight_gradient(spectrum, slope_spectrum, jnp.int32(0))
    return (activated, grad_spectral, grad_point, grad_bias)
```

```python
import jax
import jax.numpy as jnp
from jax import lax
from jax.sharding import PartitionSpec as P

MX = 32
MY = 32
MZ = 32
NY = 128
NZ = 256


HIGHEST = lax.Precision.HIGH
INV_SQRT_TWO = 0.7071067811865476
INV_SQRT_TWO_PI = 0.3989422804014327


def trig_tables(positions, frequency, length):
    product = positions[:, None] * frequency[None, :] % length
    phase_angle = 2.0 * jnp.pi / length * product.astype(jnp.float32)
    return (jnp.cos(phase_angle), jnp.sin(phase_angle))


def kept_frequencies(kept_count, length):
    mode_index = jnp.arange(kept_count, dtype=jnp.int32)
    return jnp.where(mode_index < kept_count // 2, mode_index, length - kept_count + mode_index)


def forward_local(field_in):
    channels = field_in.shape[0]
    width_x = field_in.shape[1]
    cos_z, sin_z = trig_tables(jnp.arange(NZ, dtype=jnp.int32), jnp.arange(MZ, dtype=jnp.int32), NZ)
    table_z = jnp.concatenate([cos_z, -sin_z], axis=1)
    along_z = jnp.einsum("cxyz,zk->cxyk", field_in, table_z, precision=HIGHEST)
    z_real = along_z[..., :MZ]
    z_imag = along_z[..., MZ:]
    cos_y, sin_y = trig_tables(jnp.arange(NY, dtype=jnp.int32), kept_frequencies(MY, NY), NY)
    y_real = jnp.einsum("cxyk,yj->xcjk", z_real, cos_y, precision=HIGHEST) + jnp.einsum(
        "cxyk,yj->xcjk", z_imag, sin_y, precision=HIGHEST
    )
    y_imag = jnp.einsum("cxyk,yj->xcjk", z_imag, cos_y, precision=HIGHEST) - jnp.einsum(
        "cxyk,yj->xcjk", z_real, sin_y, precision=HIGHEST
    )
    stacked = jnp.stack([y_real, y_imag], axis=1)
    return stacked.reshape(width_x, 2, channels, MY * MZ)


def transform_x(x_lines):
    length_x = x_lines.shape[0]
    cos_x, sin_x = trig_tables(
        jnp.arange(length_x, dtype=jnp.int32), kept_frequencies(MX, length_x), length_x
    )
    norm_scale = 1.0 / float(length_x * NY * NZ) ** 0.5
    part_real = x_lines[:, 0]
    part_imag = x_lines[:, 1]
    x_real = jnp.einsum("xcm,xk->kcm", part_real, cos_x, precision=HIGHEST) + jnp.einsum(
        "xcm,xk->kcm", part_imag, sin_x, precision=HIGHEST
    )
    x_imag = jnp.einsum("xcm,xk->kcm", part_imag, cos_x, precision=HIGHEST) - jnp.einsum(
        "xcm,xk->kcm", part_real, sin_x, precision=HIGHEST
    )
    return norm_scale * jnp.stack([x_real, x_imag], axis=1)


def mix_modes(spectrum, weights):
    spec_real = spectrum[:, 0]
    spec_imag = spectrum[:, 1]
    out_real = jnp.einsum("kim,kmio->kom", spec_real, weights[0], precision=HIGHEST) - jnp.einsum(
        "kim,kmio->kom", spec_imag, weights[1], precision=HIGHEST
    )
    out_imag = jnp.einsum("kim,kmio->kom", spec_real, weights[1], precision=HIGHEST) + jnp.einsum(
        "kim,kmio->kom", spec_imag, weights[0], precision=HIGHEST
    )
    return jnp.stack([out_real, out_imag], axis=1)


def inverse_x(spectrum, positions, length_x):
    cos_x, sin_x = trig_tables(positions, kept_frequencies(MX, length_x), length_x)
    spec_real = spectrum[:, 0]
    spec_imag = spectrum[:, 1]
    a_real = jnp.einsum("kcm,xk->xcm", spec_real, cos_x, precision=HIGHEST) - jnp.einsum(
        "kcm,xk->xcm", spec_imag, sin_x, precision=HIGHEST
    )
    a_imag = jnp.einsum("kcm,xk->xcm", spec_imag, cos_x, precision=HIGHEST) + jnp.einsum(
        "kcm,xk->xcm", spec_real, sin_x, precision=HIGHEST
    )
    return jnp.stack([a_real, a_imag], axis=1)


def inverse_yz(x_lines, length_x):
    width_x = x_lines.shape[0]
    channels = x_lines.shape[2]
    mode_grid = x_lines.reshape(width_x, 2, channels, MY, MZ)
    cos_y, sin_y = trig_tables(jnp.arange(NY, dtype=jnp.int32), kept_frequencies(MY, NY), NY)
    b_real = jnp.einsum("xcjk,yj->cxyk", mode_grid[:, 0], cos_y, precision=HIGHEST) - jnp.einsum(
        "xcjk,yj->cxyk", mode_grid[:, 1], sin_y, precision=HIGHEST
    )
    b_imag = jnp.einsum("xcjk,yj->cxyk", mode_grid[:, 1], cos_y, precision=HIGHEST) + jnp.einsum(
        "xcjk,yj->cxyk", mode_grid[:, 0], sin_y, precision=HIGHEST
    )
    cos_z, sin_z = trig_tables(jnp.arange(NZ, dtype=jnp.int32), jnp.arange(MZ, dtype=jnp.int32), NZ)
    weight_z = jnp.where(jnp.arange(MZ, dtype=jnp.int32) == 0, 1.0, 2.0).astype(jnp.float32)
    table_z = jnp.concatenate([cos_z * weight_z[None, :], -sin_z * weight_z[None, :]], axis=1)
    stacked = jnp.concatenate([b_real, b_imag], axis=-1)
    result = jnp.einsum("cxyk,zk->cxyz", stacked, table_z, precision=HIGHEST)
    return result * (1.0 / float(length_x * NY * NZ) ** 0.5)


def gelu_slope(values):
    return (
        0.5 * (1.0 + lax.erf(values * INV_SQRT_TWO))
        + values * jnp.exp(-0.5 * values * values) * INV_SQRT_TWO_PI
    )


def weight_gradient(spectrum, slope_modes, first_mode):
    mode_ids = first_mode + jnp.arange(spectrum.shape[3], dtype=jnp.int32)
    weight_modes = jnp.where(mode_ids % MZ == 0, 1.0, 2.0).astype(jnp.float32)
    grad_real = jnp.einsum(
        "kim,kom->kmio", spectrum[:, 0], slope_modes[:, 0], precision=HIGHEST
    ) + jnp.einsum("kim,kom->kmio", spectrum[:, 1], slope_modes[:, 1], precision=HIGHEST)
    grad_imag = jnp.einsum(
        "kim,kom->kmio", spectrum[:, 0], slope_modes[:, 1], precision=HIGHEST
    ) - jnp.einsum("kim,kom->kmio", spectrum[:, 1], slope_modes[:, 0], precision=HIGHEST)
    stacked = jnp.stack([grad_real, grad_imag], axis=0)
    return stacked * weight_modes[None, None, :, None, None]


def to_modes(field_in):
    return transform_x(
        lax.all_to_all(forward_local(field_in), "space", split_axis=3, concat_axis=0, tiled=True)
    )


def body(lifted_field, cotangent, spectral_weights, point_weights, point_bias):
    devices = lax.axis_size("space")
    width_x = lifted_field.shape[1]
    length_x = width_x * devices
    spectrum = to_modes(lifted_field)
    mixed_modes = mix_modes(spectrum, spectral_weights)
    full_lines = inverse_x(mixed_modes, jnp.arange(length_x, dtype=jnp.int32), length_x)
    spectral = inverse_yz(
        lax.all_to_all(full_lines, "space", split_axis=0, concat_axis=3, tiled=True), length_x
    )
    pointwise = (
        jnp.einsum("ixyz,io->oxyz", lifted_field, point_weights, precision=HIGHEST)
        + point_bias[:, None, None, None]
    )
    before = spectral + pointwise
    activated = jax.nn.gelu(before, approximate=False).astype(jnp.bfloat16)
    slope_field = cotangent.astype(jnp.float32) * gelu_slope(before)
    local_point = jnp.einsum("ixyz,oxyz->io", lifted_field, slope_field, precision=HIGHEST)
    local_bias = jnp.sum(slope_field, axis=(1, 2, 3))
    partial = jnp.concatenate([local_point, local_bias[None, :]], axis=0)
    copies = jnp.broadcast_to(partial[None], (devices,) + partial.shape)
    summed = jnp.sum(
        lax.all_to_all(copies, "space", split_axis=0, concat_axis=0, tiled=True), axis=0
    )
    summed_point, summed_bias = summed[:-1], summed[-1]
    root_cells = float(length_x * NY * NZ) ** 0.5
    slope_spectrum = to_modes(slope_field)
    first_mode = lax.axis_index("space") * spectrum.shape[3]
    grad_spectral = weight_gradient(spectrum, slope_spectrum, first_mode)
    return (activated, grad_spectral, summed_point / root_cells, summed_bias / root_cells)


def solution(mesh):
    placed = (
        P("groups", "space", None, None),
        P("groups", "space", None, None),
        P(None, None, "space", None, None),
        P(),
        P(),
    )
    return jax.shard_map(
        body,
        mesh=mesh,
        in_specs=placed,
        out_specs=(
            P("groups", "space", None, None),
            P("groups", None, "space", None, None),
            P("groups", None),
            P("groups"),
        ),
        check_vma=False,
    )
```

```python
import functools

import jax
import jax.numpy as jnp
import numpy as np
from jax import lax
from jax.experimental import pallas as pl
from jax.experimental.pallas import tpu as pltpu
from jax.sharding import PartitionSpec as P

MX = 32
MY = 32
MZ = 32
ROWS = 8
STEP = 16

HIGH = lax.Precision.HIGH
INV_SQRT_TWO = 0.7071067811865476
INV_SQRT_TWO_PI = 0.3989422804014327


def angles(positions, frequency, length):
    product = np.outer(np.asarray(positions), np.asarray(frequency)) % length
    phase = 2.0 * np.pi / length * product.astype(np.float64)
    return np.cos(phase), np.sin(phase)


def kept(count, length):
    index = np.arange(count)
    return np.where(index < count // 2, index, length - count + index)


def halves(table):
    table = np.asarray(table, np.float32)
    high = table.astype(jnp.bfloat16)
    low = (table - high.astype(np.float32)).astype(jnp.bfloat16)
    return jnp.asarray(high), jnp.asarray(low)


def split(value):
    high = value.astype(jnp.bfloat16)
    low = (value - high.astype(jnp.float32)).astype(jnp.bfloat16)
    return high, low


def dot3(a, b, dims=(((1,), (0,)), ((), ()))):
    one = functools.partial(
        lax.dot_general, dimension_numbers=dims, preferred_element_type=jnp.float32
    )
    return one(a[0], b[0]) + (one(a[0], b[1]) + one(a[1], b[0]))


def forward_tables(ny, nz):
    cos_z, sin_z = angles(np.arange(nz), np.arange(MZ), nz)
    table_z = np.concatenate([cos_z, -sin_z, -sin_z, -cos_z], axis=1)
    cos_y, sin_y = angles(np.arange(ny), kept(MY, ny), ny)
    table_y = np.concatenate([cos_y.T, sin_y.T], axis=0)
    return halves(table_z) + halves(table_y)


def inverse_tables(ny, nz, scale):
    cos_z, sin_z = angles(np.arange(nz), np.arange(MZ), nz)
    weight = np.where(np.arange(MZ) == 0, 1.0, 2.0)[:, None] * scale
    table = np.concatenate([cos_z.T * weight, -sin_z.T * weight], axis=0)
    blocks = np.kron(np.eye(4), table)
    cos_y, sin_y = angles(np.arange(ny), kept(MY, ny), ny)
    table_y = np.concatenate([cos_y, -sin_y], axis=1)
    return halves(blocks) + halves(table_y)


def finish_y(lines, ty, modes_ref):
    def one(c, carry):
        both = dot3(ty, split(lines[c]))
        turned = pltpu.roll(both[MY:], 2 * MZ, 1)
        modes_ref[c] = (both[:MY] + turned)[:, : 2 * MZ]
        return carry

    lax.fori_loop(0, lines.shape[0], one, 0, unroll=4)


def forward_kernel(x_ref, tzh, tzl, tyh, tyl, modes_ref, lines):
    step = pl.program_id(1)
    channels, rows, nz = x_ref.shape
    value = x_ref[...].reshape(channels * rows, nz)
    along = dot3(split(value), (tzh[...], tzl[...]))
    start = pl.multiple_of(step * rows, rows)
    lines[:, pl.ds(start, rows), :] = along.reshape(channels, rows, 4 * MZ)

    @pl.when(step == pl.num_programs(1) - 1)
    def _():
        finish_y(lines, (tyh[...], tyl[...]), modes_ref)


def whole(array):
    shape = array.shape
    return pl.BlockSpec(shape, lambda *_: (0,) * len(shape))


def field_spec(channels, nz):
    return pl.BlockSpec((channels, None, STEP, nz), lambda x, y: (0, x, y, 0))


def modes_spec(channels):
    return pl.BlockSpec((None, channels, MY, 2 * MZ), lambda x, y: (x, 0, 0, 0))


def forward_modes(field):
    channels, width, ny, nz = field.shape
    tables = forward_tables(ny, nz)
    return pl.pallas_call(
        forward_kernel,
        grid=(width, ny // STEP),
        out_shape=jax.ShapeDtypeStruct((width, channels, MY, 2 * MZ), jnp.float32),
        in_specs=[field_spec(channels, nz)] + [whole(t) for t in tables],
        out_specs=modes_spec(channels),
        scratch_shapes=[pltpu.VMEM((channels, ny, 4 * MZ), jnp.float32)],
        name="forward_modes",
    )(field, *tables)


def middle_kernel(
    m_ref, x_ref, cot_ref, wk_ref, bias_ref, bdh, bdl, iyh, iyl, tzh, tzl, tyh, tyl,
    act_ref, modes_ref, point_ref, lines, inverse, wh, wl, total,
):
    step = pl.program_id(1)
    channels, rows, nz = x_ref.shape
    quads = channels // 4
    width = 8 * MZ

    @pl.when(step == 0)
    def _():
        for part in range(0, m_ref.shape[1], 512):
            lanes = pl.ds(part, 512)
            inverse[:, lanes] = dot3((iyh[...], iyl[...]), split(m_ref[:, lanes]))
        high, low = split(wk_ref[...])
        wh[...] = high
        wl[...] = low
        total[...] = jnp.zeros_like(total)

    for half in range(rows // ROWS):
        start = pl.multiple_of(step * rows + half * ROWS, ROWS)
        stacked = jnp.concatenate(
            [inverse[pl.ds(start, ROWS), g * width : (g + 1) * width] for g in range(quads)], axis=0
        )
        spectral = dot3(split(stacked), (bdh[...], bdl[...]))
        spectral = jnp.concatenate(
            [
                spectral[g * ROWS : (g + 1) * ROWS, c * nz : (c + 1) * nz]
                for g in range(quads)
                for c in range(4)
            ],
            axis=0,
        )
        field = x_ref[:, half * ROWS : (half + 1) * ROWS, :].reshape(channels * ROWS, nz)
        field = split(field)
        before = spectral + dot3((wh[...], wl[...]), field) + bias_ref[...]
        normal = 0.5 * (1.0 + lax.erf(before * INV_SQRT_TWO))
        density = jnp.exp(-0.5 * before * before) * INV_SQRT_TWO_PI
        act_ref[:, half * ROWS : (half + 1) * ROWS, :] = (
            (before * normal).reshape(channels, ROWS, nz).astype(jnp.bfloat16)
        )
        cot = cot_ref[:, half * ROWS : (half + 1) * ROWS, :].astype(jnp.float32)
        slope = cot.reshape(channels * ROWS, nz) * (normal + before * density)
        slope = split(slope)
        total[...] += dot3(field, slope, (((1,), (1,)), ((), ())))
        along = dot3(slope, (tzh[...], tzl[...]))
        lines[:, pl.ds(start, ROWS), :] = along.reshape(channels, ROWS, 4 * MZ)

    @pl.when(step == pl.num_programs(1) - 1)
    def _():
        finish_y(lines, (tyh[...], tyl[...]), modes_ref)
        size = channels * ROWS
        row = lax.broadcasted_iota(jnp.int32, (size, size), 0) % ROWS
        column = lax.broadcasted_iota(jnp.int32, (size, size), 1) % ROWS
        diagonal = jnp.where(row == column, total[...], 0.0)
        point_ref[...] = jnp.sum(diagonal.reshape(channels, ROWS, size), axis=1)


def middle(grid_modes, field, cotangent, point_weights, point_bias, scale):
    channels, width, ny, nz = field.shape
    size = channels * ROWS
    tables = inverse_tables(ny, nz, scale) + forward_tables(ny, nz)
    eye = jnp.eye(ROWS, dtype=jnp.float32)
    wide = (point_weights.T[:, None, :, None] * eye[None, :, None, :]).reshape(size, size)
    bias = jnp.broadcast_to(jnp.repeat(point_bias, ROWS)[:, None], (size, nz))
    spec = field_spec(channels, nz)
    mixed_spec = pl.BlockSpec((None,) + grid_modes.shape[1:], lambda x, y: (x, 0, 0))
    return pl.pallas_call(
        middle_kernel,
        grid=(width, ny // STEP),
        out_shape=(
            jax.ShapeDtypeStruct(field.shape, jnp.bfloat16),
            jax.ShapeDtypeStruct((width, channels, MY, 2 * MZ), jnp.float32),
            jax.ShapeDtypeStruct((width, channels, size), jnp.float32),
        ),
        in_specs=[mixed_spec, spec, spec, whole(wide), whole(bias)] + [whole(t) for t in tables],
        out_specs=(
            spec,
            modes_spec(channels),
            pl.BlockSpec((None, channels, size), lambda x, y: (x, 0, 0)),
        ),
        scratch_shapes=[
            pltpu.VMEM((channels, ny, 4 * MZ), jnp.float32),
            pltpu.VMEM((ny, channels * 2 * MZ), jnp.float32),
            pltpu.VMEM((size, size), jnp.bfloat16),
            pltpu.VMEM((size, size), jnp.bfloat16),
            pltpu.VMEM((size, size), jnp.float32),
        ],
        name="middle",
    )(grid_modes, field, cotangent, wide, bias, *tables)


def gradient_kernel(s_ref, d_ref, out_ref):
    channels = s_ref.shape[1]
    d_real = d_ref[0]
    d_imag = d_ref[1]
    for i in range(channels):
        s_real = s_ref[0, i : i + 1, :]
        s_imag = s_ref[1, i : i + 1, :]
        out_ref[0, i] = s_real * d_real + s_imag * d_imag
        out_ref[1, i] = s_real * d_imag - s_imag * d_real


def weight_gradient(spectrum, slope_modes):
    _, kx, channels, modes = spectrum.shape
    spec = pl.BlockSpec((2, None, channels, modes), lambda k: (0, k, 0, 0))
    out = pl.pallas_call(
        gradient_kernel,
        grid=(kx,),
        out_shape=jax.ShapeDtypeStruct((2, kx, channels, channels, modes), jnp.float32),
        in_specs=[spec, spec],
        out_specs=pl.BlockSpec((2, None, channels, channels, modes), lambda k: (0, k, 0, 0, 0)),
        name="weight_gradient",
    )(spectrum, slope_modes)
    return out.transpose(0, 1, 4, 2, 3)


def x_table(length_x):
    return angles(np.arange(length_x), kept(MX, length_x), length_x)


def to_spectrum(modes, scale):
    width, channels = modes.shape[:2]
    lines = modes.reshape(width, channels, MY, 2, MZ).transpose(0, 3, 1, 2, 4)
    lines = lines.reshape(width, 2, channels, MY * MZ)
    lines = lax.all_to_all(lines, "space", split_axis=3, concat_axis=0, tiled=True)
    cos_x, sin_x = x_table(lines.shape[0])
    table = np.stack([np.stack([cos_x, -sin_x], 1), np.stack([sin_x, cos_x], 1)], 1)
    table = jnp.asarray((table * scale).astype(np.float32))
    return jnp.einsum("xrcm,xrqk->qkcm", lines, table, precision=HIGH)


def mix_modes(spectrum, weights):
    real, imag = spectrum[0], spectrum[1]
    out_real = jnp.einsum("kim,kmio->kom", real, weights[0], precision=HIGH) - jnp.einsum(
        "kim,kmio->kom", imag, weights[1], precision=HIGH
    )
    out_imag = jnp.einsum("kim,kmio->kom", real, weights[1], precision=HIGH) + jnp.einsum(
        "kim,kmio->kom", imag, weights[0], precision=HIGH
    )
    return jnp.stack([out_real, out_imag], axis=0)


def to_grid(mixed, length_x):
    channels = mixed.shape[2]
    cos_x, sin_x = x_table(length_x)
    table = np.stack([np.stack([cos_x, sin_x], 0), np.stack([-sin_x, cos_x], 0)], 0)
    table = jnp.asarray(table.astype(np.float32))
    lines = jnp.einsum("rkom,rqxk->xqom", mixed, table, precision=HIGH)
    lines = lax.all_to_all(lines, "space", split_axis=0, concat_axis=3, tiled=True)
    grid = lines.reshape(lines.shape[0], 2, channels, MY, MZ).transpose(0, 1, 3, 2, 4)
    real, imag = grid[:, 0], grid[:, 1]
    stacked = jnp.stack([jnp.stack([real, imag], 3), jnp.stack([imag, -real], 3)], 1)
    return stacked.reshape(lines.shape[0], 2 * MY, channels * 2 * MZ)


def body(lifted_field, cotangent, spectral_weights, point_weights, point_bias):
    devices = lax.axis_size("space")
    channels, width, ny, nz = lifted_field.shape
    length_x = width * devices
    scale = 1.0 / float(length_x * ny * nz) ** 0.5
    spectrum = to_spectrum(forward_modes(lifted_field), scale)
    grid_modes = to_grid(mix_modes(spectrum, spectral_weights), length_x)
    activated, slope_modes, wide_point = middle(
        grid_modes, lifted_field, cotangent, point_weights, point_bias, scale
    )
    local_point = jnp.sum(wide_point.reshape(width, channels, channels, ROWS), axis=(0, 3))
    local_bias = jnp.sum(slope_modes[:, :, 0, 0], axis=0)
    partial = jnp.concatenate([local_point, local_bias[None, :]], axis=0)
    copies = jnp.broadcast_to(partial[None], (devices,) + partial.shape)
    summed = jnp.sum(
        lax.all_to_all(copies, "space", split_axis=0, concat_axis=0, tiled=True), axis=0
    )
    slope_spectrum = to_spectrum(slope_modes, scale)
    local_modes = spectrum.shape[3]
    mode_ids = lax.axis_index("space") * local_modes + jnp.arange(local_modes, dtype=jnp.int32)
    weight_modes = jnp.where(mode_ids % MZ == 0, 1.0, 2.0).astype(jnp.float32)
    grad_spectral = weight_gradient(spectrum, slope_spectrum * weight_modes)
    return (activated, grad_spectral, summed[:-1] * scale, summed[-1] * scale)


def solution(mesh):
    placed = (
        P("groups", "space", None, None),
        P("groups", "space", None, None),
        P(None, None, "space", None, None),
        P(),
        P(),
    )
    return jax.shard_map(
        body,
        mesh=mesh,
        in_specs=placed,
        out_specs=(
            P("groups", "space", None, None),
            P("groups", None, "space", None, None),
            P("groups", None),
            P("groups"),
        ),
        check_vma=False,
    )
```

```python
import functools

import jax
import jax.numpy as jnp
import numpy as np
from jax import lax
from jax.experimental import pallas as pl
from jax.experimental.pallas import tpu as pltpu
from jax.sharding import PartitionSpec as P

MX = 32
MY = 32
MZ = 32
ROWS = 8
STEP = 32

HIGH = lax.Precision.HIGH
INV_SQRT_TWO = 0.7071067811865476
INV_SQRT_TWO_PI = 0.3989422804014327


def angles(positions, frequency, length):
    product = np.outer(np.asarray(positions), np.asarray(frequency)) % length
    phase = 2.0 * np.pi / length * product.astype(np.float64)
    return np.cos(phase), np.sin(phase)


def kept(count, length):
    index = np.arange(count)
    return np.where(index < count // 2, index, length - count + index)


def halves(table):
    table = np.asarray(table, np.float32)
    high = table.astype(jnp.bfloat16)
    low = (table - high.astype(np.float32)).astype(jnp.bfloat16)
    return jnp.asarray(high), jnp.asarray(low)


def split(value):
    high = value.astype(jnp.bfloat16)
    low = (value - high.astype(jnp.float32)).astype(jnp.bfloat16)
    return high, low


def dot3(a, b, dims=(((1,), (0,)), ((), ()))):
    one = functools.partial(
        lax.dot_general, dimension_numbers=dims, preferred_element_type=jnp.float32
    )
    return one(a[0], b[0]) + (one(a[0], b[1]) + one(a[1], b[0]))


def forward_tables(ny, nz):
    cos_z, sin_z = angles(np.arange(nz), np.arange(MZ), nz)
    table_z = np.concatenate([cos_z, -sin_z, -sin_z, -cos_z], axis=1)
    cos_y, sin_y = angles(np.arange(ny), kept(MY, ny), ny)
    table_y = np.concatenate([cos_y.T, sin_y.T], axis=0)
    return halves(table_z) + halves(table_y)


def inverse_tables(ny, nz, scale, local_rows):
    cos_z, sin_z = angles(np.arange(nz), np.arange(MZ), nz)
    weight = np.where(np.arange(MZ) == 0, 1.0, 2.0)[:, None] * scale
    real = np.kron(np.eye(4), cos_z.T * weight)
    imag = np.kron(np.eye(4), -sin_z.T * weight)
    cos_y, sin_y = angles(np.arange(ny), kept(MY, ny), ny)
    cos_y = cos_y.reshape(ny, MY // local_rows, local_rows)
    sin_y = sin_y.reshape(ny, MY // local_rows, local_rows)
    real_y = np.stack([cos_y, -sin_y], 2).reshape(ny, 2 * MY)
    imag_y = np.stack([sin_y, cos_y], 2).reshape(ny, 2 * MY)
    return halves(np.concatenate([real, imag], 0)) + halves(np.concatenate([real_y, imag_y], 0))


def finish_y(lines, ty, modes_ref):
    def one(c, carry):
        both = dot3(ty, split(lines[c]))
        turned = pltpu.roll(both[MY:], 2 * MZ, 1)
        modes_ref[c] = (both[:MY] + turned)[:, : 2 * MZ]
        return carry

    lax.fori_loop(0, lines.shape[0], one, 0, unroll=16)


def forward_kernel(x_ref, tzh, tzl, tyh, tyl, modes_ref, lines):
    step = pl.program_id(1)
    channels, rows, nz = x_ref.shape
    value = x_ref[...].reshape(channels * rows, nz)
    along = dot3(split(value), (tzh[...], tzl[...]))
    start = pl.multiple_of(step * rows, rows)
    lines[:, pl.ds(start, rows), :] = along.reshape(channels, rows, 4 * MZ)

    @pl.when(step == pl.num_programs(1) - 1)
    def _():
        finish_y(lines, (tyh[...], tyl[...]), modes_ref)


def whole(array):
    shape = array.shape
    return pl.BlockSpec(shape, lambda *_: (0,) * len(shape))


def field_spec(channels, nz):
    return pl.BlockSpec((channels, None, STEP, nz), lambda x, y: (0, x, y, 0))


def modes_spec(channels):
    return pl.BlockSpec((None, channels, MY, 2 * MZ), lambda x, y: (x, 0, 0, 0))


def forward_modes(field):
    channels, width, ny, nz = field.shape
    tables = forward_tables(ny, nz)
    return pl.pallas_call(
        forward_kernel,
        grid=(width, ny // STEP),
        out_shape=jax.ShapeDtypeStruct((width, channels, MY, 2 * MZ), jnp.float32),
        in_specs=[field_spec(channels, nz)] + [whole(t) for t in tables],
        out_specs=modes_spec(channels),
        scratch_shapes=[pltpu.VMEM((channels, ny, 4 * MZ), jnp.float32)],
        name="forward_modes",
    )(field, *tables)


def middle_kernel(
    m_ref, x_ref, cot_ref, w_ref, bias_ref, pick, bdh, bdl, iyh, iyl, tzh, tzl, tyh, tyl,
    act_ref, modes_ref, point_ref, lines, inverse, field_part, wh, wl, total,
):
    step = pl.program_id(1)
    channels, rows, nz = x_ref.shape
    quads = channels // 4
    width = 4 * MZ
    ny = lines.shape[1]

    def same_row():
        size = channels * ROWS
        row = lax.broadcasted_iota(jnp.int32, (size, size), 0) % ROWS
        column = lax.broadcasted_iota(jnp.int32, (size, size), 1) % ROWS
        return row == column

    @pl.when(step == 0)
    def _():
        for part in range(0, m_ref.shape[1], 256):
            lanes = pl.ds(part, 256)
            both = dot3((iyh[...], iyl[...]), split(m_ref[:, lanes]))
            inverse[0, :, lanes] = both[:ny]
            inverse[1, :, lanes] = both[ny:]
        contract = (((1,), (1,)), ((), ()))
        for narrow, out in zip(split(w_ref[...]), (wh, wl)):
            tall = lax.dot_general(
                pick[...], narrow, contract, preferred_element_type=jnp.float32
            ).astype(jnp.bfloat16)
            square = lax.dot_general(tall, pick[...], contract, preferred_element_type=jnp.float32)
            out[...] = jnp.where(same_row(), square, 0.0).astype(jnp.bfloat16)
        total[...] = jnp.zeros_like(total)

    first = pl.multiple_of(step * rows, rows)
    stacked = jnp.concatenate(
        [
            jnp.concatenate(
                [
                    inverse[r, pl.ds(first, rows), g * width : (g + 1) * width]
                    for r in range(2)
                ],
                axis=1,
            )
            for g in range(quads)
        ],
        axis=0,
    )
    stacked = split(stacked)
    for c in range(4):
        lanes = slice(c * nz, (c + 1) * nz)
        field_part[:, lanes] = dot3(stacked, (bdh[:, lanes], bdl[:, lanes]))

    for half in range(rows // ROWS):
        here = slice(half * ROWS, (half + 1) * ROWS)
        start = pl.multiple_of(step * rows + half * ROWS, ROWS)
        spectral = jnp.concatenate(
            [
                field_part[
                    g * rows + half * ROWS : g * rows + (half + 1) * ROWS, c * nz : (c + 1) * nz
                ]
                for g in range(quads)
                for c in range(4)
            ],
            axis=0,
        )
        field = split(x_ref[:, here, :].reshape(channels * ROWS, nz))
        before = spectral + dot3((wh[...], wl[...]), field)
        before = before.reshape(channels, ROWS, nz) + bias_ref[...]
        normal = 0.5 * (1.0 + lax.erf(before * INV_SQRT_TWO))
        density = jnp.exp(-0.5 * before * before) * INV_SQRT_TWO_PI
        act_ref[:, here, :] = (before * normal).astype(jnp.bfloat16)
        slope = cot_ref[:, here, :].astype(jnp.float32) * (normal + before * density)
        slope = split(slope.reshape(channels * ROWS, nz))
        total[...] += dot3(field, slope, (((1,), (1,)), ((), ())))
        along = dot3(slope, (tzh[...], tzl[...]))
        lines[:, pl.ds(start, ROWS), :] = along.reshape(channels, ROWS, 4 * MZ)

    @pl.when(step == pl.num_programs(1) - 1)
    def _():
        finish_y(lines, (tyh[...], tyl[...]), modes_ref)
        size = channels * ROWS
        diagonal = jnp.where(same_row(), total[...], 0.0)
        point_ref[...] = jnp.sum(diagonal.reshape(channels, ROWS, size), axis=1)


def middle(grid_modes, local_rows, field, cotangent, point_weights, point_bias, scale):
    channels, width, ny, nz = field.shape
    size = channels * ROWS
    tables = inverse_tables(ny, nz, scale, local_rows) + forward_tables(ny, nz)
    pick = jnp.asarray(np.repeat(np.eye(channels, dtype=np.float32), ROWS, 0).astype(jnp.bfloat16))
    bias = jnp.broadcast_to(point_bias[:, None, None], (channels, 1, nz))
    spec = field_spec(channels, nz)
    mixed_spec = pl.BlockSpec((None,) + grid_modes.shape[1:], lambda x, y: (x, 0, 0))
    return pl.pallas_call(
        middle_kernel,
        grid=(width, ny // STEP),
        out_shape=(
            jax.ShapeDtypeStruct(field.shape, jnp.bfloat16),
            jax.ShapeDtypeStruct((width, channels, MY, 2 * MZ), jnp.float32),
            jax.ShapeDtypeStruct((width, channels, size), jnp.float32),
        ),
        in_specs=[mixed_spec, spec, spec, whole(point_weights), whole(bias), whole(pick)]
        + [whole(t) for t in tables],
        out_specs=(
            spec,
            modes_spec(channels),
            pl.BlockSpec((None, channels, size), lambda x, y: (x, 0, 0)),
        ),
        scratch_shapes=[
            pltpu.VMEM((channels, ny, 4 * MZ), jnp.float32),
            pltpu.VMEM((2, ny, channels * MZ), jnp.float32),
            pltpu.VMEM((channels // 4 * STEP, 4 * nz), jnp.float32),
            pltpu.VMEM((size, size), jnp.bfloat16),
            pltpu.VMEM((size, size), jnp.bfloat16),
            pltpu.VMEM((size, size), jnp.float32),
        ],
        name="middle",
    )(grid_modes, field, cotangent, point_weights, bias, pick, *tables)


def weight_gradient(spectrum, slope_modes):
    turned = jnp.stack([slope_modes[1], -slope_modes[0]], axis=0)
    slope_modes, turned = lax.optimization_barrier((slope_modes, turned))
    real = spectrum[0][None, :, :, None, :]
    imag = spectrum[1][None, :, :, None, :]
    out = real * slope_modes[:, :, None] + imag * turned[:, :, None]
    return out.transpose(0, 1, 4, 2, 3)


def x_table(length_x):
    return angles(np.arange(length_x), kept(MX, length_x), length_x)


def exchange(lines):
    return lax.all_to_all(lines, "space", split_axis=0, concat_axis=0, tiled=True)


def to_spectrum(modes, scale, devices, extra=None):
    width, channels = modes.shape[:2]
    local = MY * MZ // devices
    lines = modes.reshape(width, channels, MY, 2, MZ).transpose(0, 3, 1, 2, 4)
    lines = lines.reshape(width, 2, channels, devices, local).transpose(3, 0, 1, 2, 4)
    lines = lines.reshape(devices, width * 2 * channels * local)
    size = lines.shape[1]
    if extra is not None:
        extra = jnp.pad(extra, (0, -extra.shape[0] % 128))
        extra = jnp.broadcast_to(extra[None], (devices,) + extra.shape)
        lines = jnp.concatenate([lines, extra], axis=1)
    lines = exchange(lines)
    summed = jnp.sum(lines[:, size:], axis=0)
    lines = lines[:, :size].reshape(devices * width, 2, channels, local)
    cos_x, sin_x = x_table(devices * width)
    table = np.stack([np.stack([cos_x, -sin_x], 1), np.stack([sin_x, cos_x], 1)], 1)
    table = jnp.asarray((table * scale).astype(np.float32))
    return jnp.einsum("xrcm,xrqk->qkcm", lines, table, precision=HIGH), summed


def mix_modes(spectrum, weights):
    real, imag = spectrum[0], spectrum[1]
    out_real = jnp.einsum("kim,kmio->kom", real, weights[0], precision=HIGH) - jnp.einsum(
        "kim,kmio->kom", imag, weights[1], precision=HIGH
    )
    out_imag = jnp.einsum("kim,kmio->kom", real, weights[1], precision=HIGH) + jnp.einsum(
        "kim,kmio->kom", imag, weights[0], precision=HIGH
    )
    return jnp.stack([out_real, out_imag], axis=0)


def to_grid(mixed, length_x):
    channels = mixed.shape[2]
    cos_x, sin_x = x_table(length_x)
    table = np.stack([np.stack([cos_x, sin_x], 0), np.stack([-sin_x, cos_x], 0)], 0)
    table = jnp.asarray(table.astype(np.float32))
    lines = jnp.einsum("rkom,rqxk->xqom", mixed, table, precision=HIGH)
    local = mixed.shape[3]
    devices = MY * MZ // local
    width = length_x // devices
    if local % MZ == 0:
        local_rows = local // MZ
        lines = lines.reshape(length_x, 2, channels, local_rows, MZ).transpose(0, 1, 3, 2, 4)
        lines = exchange(lines.reshape(length_x, 2 * local_rows * channels * MZ))
        grid = lines.reshape(devices, width, 2 * local_rows, channels * MZ).transpose(1, 0, 2, 3)
    else:
        local_rows = 1
        lines = exchange(lines.reshape(length_x, 2 * channels * local))
        grid = lines.reshape(MY, MZ // local, width, 2, channels, local).transpose(2, 0, 3, 4, 1, 5)
    return grid.reshape(width, 2 * MY, channels * MZ), local_rows


def body(lifted_field, cotangent, spectral_weights, point_weights, point_bias):
    devices = lax.axis_size("space")
    channels, width, ny, nz = lifted_field.shape
    length_x = width * devices
    scale = 1.0 / float(length_x * ny * nz) ** 0.5
    spectrum, _ = to_spectrum(forward_modes(lifted_field), scale, devices)
    grid_modes, local_rows = to_grid(mix_modes(spectrum, spectral_weights), length_x)
    activated, slope_modes, wide_point = middle(
        grid_modes, local_rows, lifted_field, cotangent, point_weights, point_bias, scale
    )
    local_point = jnp.sum(wide_point.reshape(width, channels, channels, ROWS), axis=(0, 3))
    local_bias = jnp.sum(slope_modes[:, :, 0, 0], axis=0)
    partial = jnp.concatenate([local_point.reshape(-1), local_bias])
    slope_spectrum, summed = to_spectrum(slope_modes, scale, devices, partial)
    area = channels * channels
    summed_point = summed[:area].reshape(channels, channels)
    summed_bias = summed[area : area + channels]
    local_modes = spectrum.shape[3]
    mode_ids = lax.axis_index("space") * local_modes + jnp.arange(local_modes, dtype=jnp.int32)
    weight_modes = jnp.where(mode_ids % MZ == 0, 1.0, 2.0).astype(jnp.float32)
    grad_spectral = weight_gradient(spectrum, slope_spectrum * weight_modes)
    return (activated, grad_spectral, summed_point * scale, summed_bias * scale)


def solution(mesh):
    placed = (
        P("groups", "space", None, None),
        P("groups", "space", None, None),
        P(None, None, "space", None, None),
        P(),
        P(),
    )
    return jax.shard_map(
        body,
        mesh=mesh,
        in_specs=placed,
        out_specs=(
            P("groups", "space", None, None),
            P("groups", None, "space", None, None),
            P("groups", None),
            P("groups"),
        ),
        check_vma=False,
    )
```

```python
import functools

import jax
import jax.numpy as jnp
import numpy as np
from jax import lax
from jax.experimental import pallas as pl
from jax.experimental.pallas import tpu as pltpu
from jax.sharding import PartitionSpec as P

MX = 32
MY = 32
MZ = 32
ROWS = 8
STEP = 32

HIGH = lax.Precision.HIGH
INV_SQRT_TWO = 0.7071067811865476
INV_SQRT_TWO_PI = 0.3989422804014327


def angles(positions, frequency, length):
    product = np.outer(np.asarray(positions), np.asarray(frequency)) % length
    phase = 2.0 * np.pi / length * product.astype(np.float64)
    return np.cos(phase), np.sin(phase)


def kept(count, length):
    index = np.arange(count)
    return np.where(index < count // 2, index, length - count + index)


def halves(table):
    table = np.asarray(table, np.float32)
    high = table.astype(jnp.bfloat16)
    low = (table - high.astype(np.float32)).astype(jnp.bfloat16)
    return jnp.asarray(high), jnp.asarray(low)


def split(value):
    high = value.astype(jnp.bfloat16)
    low = (value - high.astype(jnp.float32)).astype(jnp.bfloat16)
    return high, low


def dot3(a, b, dims=(((1,), (0,)), ((), ()))):
    one = functools.partial(
        lax.dot_general, dimension_numbers=dims, preferred_element_type=jnp.float32
    )
    return one(a[0], b[0]) + (one(a[0], b[1]) + one(a[1], b[0]))


def forward_tables(ny, nz):
    cos_z, sin_z = angles(np.arange(nz), np.arange(MZ), nz)
    table_z = np.concatenate([cos_z, -sin_z, -sin_z, -cos_z], axis=1)
    cos_y, sin_y = angles(np.arange(ny), kept(MY, ny), ny)
    table_y = np.concatenate([cos_y.T, sin_y.T], axis=0)
    return halves(table_z) + halves(table_y)


def inverse_tables(ny, nz, scale, local_rows):
    cos_z, sin_z = angles(np.arange(nz), np.arange(MZ), nz)
    weight = np.where(np.arange(MZ) == 0, 1.0, 2.0)[:, None] * scale
    real = np.kron(np.eye(4), cos_z.T * weight)
    imag = np.kron(np.eye(4), -sin_z.T * weight)
    cos_y, sin_y = angles(np.arange(ny), kept(MY, ny), ny)
    cos_y = cos_y.reshape(ny, MY // local_rows, local_rows)
    sin_y = sin_y.reshape(ny, MY // local_rows, local_rows)
    real_y = np.stack([cos_y, -sin_y], 2).reshape(ny, 2 * MY)
    imag_y = np.stack([sin_y, cos_y], 2).reshape(ny, 2 * MY)
    return halves(np.concatenate([real, imag], 0)) + halves(np.concatenate([real_y, imag_y], 0))


def finish_y(lines, ty, modes_ref):
    def one(c, carry):
        both = dot3(ty, split(lines[c]))
        turned = pltpu.roll(both[MY:], 2 * MZ, 1)
        modes_ref[c] = (both[:MY] + turned)[:, : 2 * MZ]
        return carry

    lax.fori_loop(0, lines.shape[0], one, 0, unroll=16)


def forward_kernel(x_ref, tzh, tzl, tyh, tyl, modes_ref, lines):
    step = pl.program_id(1)
    channels, rows, nz = x_ref.shape
    value = x_ref[...].reshape(channels * rows, nz)
    along = dot3(split(value), (tzh[...], tzl[...]))
    start = pl.multiple_of(step * rows, rows)
    lines[:, pl.ds(start, rows), :] = along.reshape(channels, rows, 4 * MZ)

    @pl.when(step == pl.num_programs(1) - 1)
    def _():
        finish_y(lines, (tyh[...], tyl[...]), modes_ref)


def whole(array):
    shape = array.shape
    return pl.BlockSpec(shape, lambda *_: (0,) * len(shape))


def field_spec(channels, nz):
    return pl.BlockSpec((channels, None, STEP, nz), lambda x, y: (0, x, y, 0))


def modes_spec(channels):
    return pl.BlockSpec((None, channels, MY, 2 * MZ), lambda x, y: (x, 0, 0, 0))


def forward_modes(field):
    channels, width, ny, nz = field.shape
    tables = forward_tables(ny, nz)
    return pl.pallas_call(
        forward_kernel,
        grid=(width, ny // STEP),
        out_shape=jax.ShapeDtypeStruct((width, channels, MY, 2 * MZ), jnp.float32),
        in_specs=[field_spec(channels, nz)] + [whole(t) for t in tables],
        out_specs=modes_spec(channels),
        scratch_shapes=[pltpu.VMEM((channels, ny, 4 * MZ), jnp.float32)],
        name="forward_modes",
    )(field, *tables)


def middle_kernel(
    m_ref, x_ref, cot_ref, w_ref, bias_ref, pick, bdh, bdl, iyh, iyl, tzh, tzl, tyh, tyl,
    act_ref, modes_ref, point_ref, lines, inverse, field_part, wh, wl, total,
):
    step = pl.program_id(1)
    channels, rows, nz = x_ref.shape
    quads = channels // 4
    width = 4 * MZ
    ny = lines.shape[1]

    def same_row():
        size = channels * ROWS
        row = lax.broadcasted_iota(jnp.int32, (size, size), 0) % ROWS
        column = lax.broadcasted_iota(jnp.int32, (size, size), 1) % ROWS
        return row == column

    @pl.when(step == 0)
    def _():
        for part in range(0, m_ref.shape[1], 256):
            lanes = pl.ds(part, 256)
            both = dot3((iyh[...], iyl[...]), split(m_ref[:, lanes]))
            inverse[0, :, lanes] = both[:ny]
            inverse[1, :, lanes] = both[ny:]
        contract = (((1,), (1,)), ((), ()))
        for narrow, out in zip(split(w_ref[...]), (wh, wl)):
            tall = lax.dot_general(
                pick[...], narrow, contract, preferred_element_type=jnp.float32
            ).astype(jnp.bfloat16)
            square = lax.dot_general(tall, pick[...], contract, preferred_element_type=jnp.float32)
            out[...] = jnp.where(same_row(), square, 0.0).astype(jnp.bfloat16)
        total[...] = jnp.zeros_like(total)

    first = pl.multiple_of(step * rows, rows)
    stacked = jnp.concatenate(
        [
            jnp.concatenate(
                [
                    inverse[r, pl.ds(first, rows), g * width : (g + 1) * width]
                    for r in range(2)
                ],
                axis=1,
            )
            for g in range(quads)
        ],
        axis=0,
    )
    stacked = split(stacked)
    for c in range(4):
        lanes = slice(c * nz, (c + 1) * nz)
        field_part[:, lanes] = dot3(stacked, (bdh[:, lanes], bdl[:, lanes]))

    for half in range(rows // ROWS):
        here = slice(half * ROWS, (half + 1) * ROWS)
        start = pl.multiple_of(step * rows + half * ROWS, ROWS)
        spectral = jnp.concatenate(
            [
                field_part[
                    g * rows + half * ROWS : g * rows + (half + 1) * ROWS, c * nz : (c + 1) * nz
                ]
                for g in range(quads)
                for c in range(4)
            ],
            axis=0,
        )
        field = split(x_ref[:, here, :].reshape(channels * ROWS, nz))
        before = spectral + dot3((wh[...], wl[...]), field)
        before = before.reshape(channels, ROWS, nz) + bias_ref[...]
        normal = 0.5 * (1.0 + lax.erf(before * INV_SQRT_TWO))
        density = jnp.exp(-0.5 * before * before) * INV_SQRT_TWO_PI
        act_ref[:, here, :] = (before * normal).astype(jnp.bfloat16)
        slope = cot_ref[:, here, :].astype(jnp.float32) * (normal + before * density)
        slope = split(slope.reshape(channels * ROWS, nz))
        total[...] += dot3(field, slope, (((1,), (1,)), ((), ())))
        along = dot3(slope, (tzh[...], tzl[...]))
        lines[:, pl.ds(start, ROWS), :] = along.reshape(channels, ROWS, 4 * MZ)

    @pl.when(step == pl.num_programs(1) - 1)
    def _():
        finish_y(lines, (tyh[...], tyl[...]), modes_ref)
        size = channels * ROWS
        diagonal = jnp.where(same_row(), total[...], 0.0)
        point_ref[...] = jnp.sum(diagonal.reshape(channels, ROWS, size), axis=1)


def middle(grid_modes, local_rows, field, cotangent, point_weights, point_bias, scale):
    channels, width, ny, nz = field.shape
    size = channels * ROWS
    tables = inverse_tables(ny, nz, scale, local_rows) + forward_tables(ny, nz)
    pick = jnp.asarray(np.repeat(np.eye(channels, dtype=np.float32), ROWS, 0).astype(jnp.bfloat16))
    bias = jnp.broadcast_to(point_bias[:, None, None], (channels, 1, nz))
    spec = field_spec(channels, nz)
    mixed_spec = pl.BlockSpec((None,) + grid_modes.shape[1:], lambda x, y: (x, 0, 0))
    return pl.pallas_call(
        middle_kernel,
        grid=(width, ny // STEP),
        out_shape=(
            jax.ShapeDtypeStruct(field.shape, jnp.bfloat16),
            jax.ShapeDtypeStruct((width, channels, MY, 2 * MZ), jnp.float32),
            jax.ShapeDtypeStruct((width, channels, size), jnp.float32),
        ),
        in_specs=[mixed_spec, spec, spec, whole(point_weights), whole(bias), whole(pick)]
        + [whole(t) for t in tables],
        out_specs=(
            spec,
            modes_spec(channels),
            pl.BlockSpec((None, channels, size), lambda x, y: (x, 0, 0)),
        ),
        scratch_shapes=[
            pltpu.VMEM((channels, ny, 4 * MZ), jnp.float32),
            pltpu.VMEM((2, ny, channels * MZ), jnp.float32),
            pltpu.VMEM((channels // 4 * STEP, 4 * nz), jnp.float32),
            pltpu.VMEM((size, size), jnp.bfloat16),
            pltpu.VMEM((size, size), jnp.bfloat16),
            pltpu.VMEM((size, size), jnp.float32),
        ],
        name="middle",
    )(grid_modes, field, cotangent, point_weights, bias, pick, *tables)


def weight_gradient(spectrum, slope_modes):
    turned = jnp.stack([slope_modes[1], -slope_modes[0]], axis=0)
    slope_modes, turned = lax.optimization_barrier((slope_modes, turned))
    real = spectrum[0][None, :, :, None, :]
    imag = spectrum[1][None, :, :, None, :]
    out = real * slope_modes[:, :, None] + imag * turned[:, :, None]
    return out.transpose(0, 1, 4, 2, 3)


def x_table(length_x):
    return angles(np.arange(length_x), kept(MX, length_x), length_x)


def exchange_kernel(devices, src, out, send_sem, recv_sem, own_sem):
    me = lax.axis_index("space")
    barrier = pltpu.get_barrier_semaphore()

    def greet(step, carry):
        peer = lax.rem(me + step, devices)
        pl.semaphore_signal(
            barrier, inc=1, device_id={"space": peer}, device_id_type=pl.DeviceIdType.MESH
        )
        return carry

    def copy(step, slot):
        peer = lax.rem(me + step, devices)
        return pltpu.make_async_remote_copy(
            src_ref=src.at[peer],
            dst_ref=out.at[slot],
            send_sem=send_sem.at[step],
            recv_sem=recv_sem.at[step],
            device_id={"space": peer},
            device_id_type=pl.DeviceIdType.MESH,
        )

    def send(step, carry):
        copy(step, me).start()
        return carry

    def finish(step, carry):
        done = copy(step, lax.rem(me + devices - step, devices))
        done.wait_send()
        done.wait_recv()
        return carry

    lax.fori_loop(1, devices, greet, 0)
    own = pltpu.make_async_copy(src.at[me], out.at[me], own_sem)
    own.start()
    pl.semaphore_wait(barrier, devices - 1)
    lax.fori_loop(1, devices, send, 0)
    own.wait()
    lax.fori_loop(1, devices, finish, 0)


def exchange(lines, identity):
    devices = lax.axis_size("space")
    shape = lines.shape
    lines = lines.reshape(devices, -1, 128)
    vmem = pl.BlockSpec(memory_space=pltpu.VMEM)
    out = pl.pallas_call(
        functools.partial(exchange_kernel, devices),
        out_shape=jax.ShapeDtypeStruct(lines.shape, jnp.float32),
        in_specs=[vmem],
        out_specs=vmem,
        scratch_shapes=[
            pltpu.SemaphoreType.DMA((devices,)),
            pltpu.SemaphoreType.DMA((devices,)),
            pltpu.SemaphoreType.DMA,
        ],
        compiler_params=pltpu.CompilerParams(collective_id=identity, has_side_effects=True),
        name=f"exchange_{identity}",
    )(lines)
    return out.reshape(shape)


def to_spectrum(modes, scale, devices, extra=None):
    width, channels = modes.shape[:2]
    local = MY * MZ // devices
    lines = modes.reshape(width, channels, MY, 2, MZ).transpose(0, 3, 1, 2, 4)
    lines = lines.reshape(width, 2, channels, devices, local).transpose(3, 0, 1, 2, 4)
    lines = lines.reshape(devices, width * 2 * channels * local)
    size = lines.shape[1]
    if extra is not None:
        extra = jnp.pad(extra, (0, -extra.shape[0] % 128))
        extra = jnp.broadcast_to(extra[None], (devices,) + extra.shape)
        lines = jnp.concatenate([lines, extra], axis=1)
    lines = exchange(lines, 0 if extra is None else 2)
    summed = jnp.sum(lines[:, size:], axis=0)
    lines = lines[:, :size].reshape(devices * width, 2, channels, local)
    cos_x, sin_x = x_table(devices * width)
    table = np.stack([np.stack([cos_x, -sin_x], 1), np.stack([sin_x, cos_x], 1)], 1)
    table = jnp.asarray((table * scale).astype(np.float32))
    return jnp.einsum("xrcm,xrqk->qkcm", lines, table, precision=HIGH), summed


def mix_modes(spectrum, weights):
    real, imag = spectrum[0], spectrum[1]
    out_real = jnp.einsum("kim,kmio->kom", real, weights[0], precision=HIGH) - jnp.einsum(
        "kim,kmio->kom", imag, weights[1], precision=HIGH
    )
    out_imag = jnp.einsum("kim,kmio->kom", real, weights[1], precision=HIGH) + jnp.einsum(
        "kim,kmio->kom", imag, weights[0], precision=HIGH
    )
    return jnp.stack([out_real, out_imag], axis=0)


def to_grid(mixed, length_x):
    channels = mixed.shape[2]
    cos_x, sin_x = x_table(length_x)
    table = np.stack([np.stack([cos_x, sin_x], 0), np.stack([-sin_x, cos_x], 0)], 0)
    table = jnp.asarray(table.astype(np.float32))
    lines = jnp.einsum("rkom,rqxk->xqom", mixed, table, precision=HIGH)
    local = mixed.shape[3]
    devices = MY * MZ // local
    width = length_x // devices
    if local % MZ == 0:
        local_rows = local // MZ
        lines = lines.reshape(length_x, 2, channels, local_rows, MZ).transpose(0, 1, 3, 2, 4)
        lines = exchange(lines.reshape(length_x, 2 * local_rows * channels * MZ), 1)
        grid = lines.reshape(devices, width, 2 * local_rows, channels * MZ).transpose(1, 0, 2, 3)
    else:
        local_rows = 1
        lines = exchange(lines.reshape(length_x, 2 * channels * local), 1)
        grid = lines.reshape(MY, MZ // local, width, 2, channels, local).transpose(2, 0, 3, 4, 1, 5)
    return grid.reshape(width, 2 * MY, channels * MZ), local_rows


def body(lifted_field, cotangent, spectral_weights, point_weights, point_bias):
    devices = lax.axis_size("space")
    channels, width, ny, nz = lifted_field.shape
    length_x = width * devices
    scale = 1.0 / float(length_x * ny * nz) ** 0.5
    spectrum, _ = to_spectrum(forward_modes(lifted_field), scale, devices)
    grid_modes, local_rows = to_grid(mix_modes(spectrum, spectral_weights), length_x)
    activated, slope_modes, wide_point = middle(
        grid_modes, local_rows, lifted_field, cotangent, point_weights, point_bias, scale
    )
    local_point = jnp.sum(wide_point.reshape(width, channels, channels, ROWS), axis=(0, 3))
    local_bias = jnp.sum(slope_modes[:, :, 0, 0], axis=0)
    partial = jnp.concatenate([local_point.reshape(-1), local_bias])
    slope_spectrum, summed = to_spectrum(slope_modes, scale, devices, partial)
    area = channels * channels
    summed_point = summed[:area].reshape(channels, channels)
    summed_bias = summed[area : area + channels]
    local_modes = spectrum.shape[3]
    mode_ids = lax.axis_index("space") * local_modes + jnp.arange(local_modes, dtype=jnp.int32)
    weight_modes = jnp.where(mode_ids % MZ == 0, 1.0, 2.0).astype(jnp.float32)
    grad_spectral = weight_gradient(spectrum, slope_spectrum * weight_modes)
    return (activated, grad_spectral, summed_point * scale, summed_bias * scale)


def solution(mesh):
    placed = (
        P("groups", "space", None, None),
        P("groups", "space", None, None),
        P(None, None, "space", None, None),
        P(),
        P(),
    )
    return jax.shard_map(
        body,
        mesh=mesh,
        in_specs=placed,
        out_specs=(
            P("groups", "space", None, None),
            P("groups", None, "space", None, None),
            P("groups", None),
            P("groups"),
        ),
        check_vma=False,
    )
```
